256 devices in a mesh: seq: 16 (over x, y), head: 16 (over z, core).
Axes of the slice: x: 4, y: 4, z: 8, core: 2. Of those that a mesh axis runs over, the one named last changes fastest.
Arguments:
- queries: bfloat16 [32768, 8192], P('seq', 'head'), may hold values from -80 to 80
- transposed_keys: bfloat16 [1024, 32768], P('head', 'seq'), may hold values from -25 to 25
- transposed_values: bfloat16 [1024, 32768], P('head', 'seq'), may hold values from -6 to 6
- adapter_down_factor: bfloat16 [8192, 64], P('head'), may hold values from -0.5 to 0.5
- adapter_up_factor: bfloat16 [64, 8192], P(None, 'head'), may hold values from -0.75 to 0.75
- projection_output_gradient: bfloat16 [32768, 8192], P('seq', 'head'), may hold values from -0.03125 to 0.03125
Outputs:
- adapter_activations: float32 [64, 32768], P(None, 'seq')
- down_factor_gradient: float32 [8192, 64], P('head')
- up_factor_gradient: float32 [64, 8192], P(None, 'head')
The draws below stay inside these ranges and needn't reach their ends.
All inputs are finite; a program needn't handle non-finite values.
Results may differ from the reference program's by a relative error of at most 0.0046.
Values may be sent and summed in bfloat16 or wider, within the bound.
No kernel may reach another device: no remote copies, remote signals or barrier semaphores. Data moves between devices by JAX's collectives and lax.ppermute only.
A program may use at most 64 MiB of HBM per device.

```python
import math
import jax
import jax.numpy as jnp
from jax import lax

GROUP = 2048
HALF = 1024
SEQ_LEN = 32768
HEAD_SIZE = 128
H = 64
KVH = 8
MODEL_WIDTH = 8192
ADAPTER_RANK = 64


def joint_draw(key):
    query_seed = jax.random.fold_in(key, 11)
    keys_seed = jax.random.fold_in(key, 23)
    base_query = jax.random.truncated_normal(query_seed, -6.0, 6.0, (SEQ_LEN, MODEL_WIDTH), jnp.float32)
    base_key = jax.random.truncated_normal(keys_seed, -6.0, 6.0, (KVH * HEAD_SIZE, SEQ_LEN), jnp.float32)
    return (base_query, base_key)


def draw_queries(key, part):
    return joint_draw(key)[0].astype(jnp.bfloat16)


def draw_transposed_keys(key, part):
    return joint_draw(key)[1].astype(jnp.bfloat16)


def level_of(rng, dims, shards, smallest, high):
    level, own = 1.0, jax.random.fold_in(rng, 6)
    for dim, blocks in shards:
        draws = jnp.exp(jax.random.uniform(jax.random.fold_in(own, dim), (blocks,), jnp.float32, smallest / len(shards), high / len(shards)))
        level = level * jnp.repeat(draws, dims[dim] // blocks).reshape([-1 if axis == dim else 1 for axis in range(len(dims))])
    return level


def gaussian(own_key, shape, scale, limit, cuts=(), held_as=jnp.bfloat16):
    gain = level_of(own_key, shape, cuts, -0.22, 0.18) if cuts else 1.0
    entries = jax.random.normal(own_key, shape, jnp.float32) * scale * gain
    return jnp.minimum(jnp.maximum(entries, -limit), limit).astype(held_as)


def setup_inputs(seed: int = 0) -> dict:
    key_of = jax.random.split(jax.random.key(seed), 7)
    return {
        "queries": draw_queries(jax.random.fold_in(key_of[6], 71), 0),
        "transposed_keys": draw_transposed_keys(jax.random.fold_in(key_of[6], 71), 0),
        "transposed_values": gaussian(key_of[2], (KVH * HEAD_SIZE, SEQ_LEN), 1.0, 6.0, ((0, 16), (1, 16))),
        "adapter_down_factor": gaussian(key_of[3], (MODEL_WIDTH, ADAPTER_RANK), HEAD_SIZE ** -0.5, 0.5, ((0, 16),)),
        "adapter_up_factor": gaussian(key_of[4], (ADAPTER_RANK, MODEL_WIDTH), ADAPTER_RANK ** -0.5, 0.75, ((1, 16),)),
        "projection_output_gradient": gaussian(key_of[5], (SEQ_LEN, MODEL_WIDTH), SEQ_LEN ** -0.5, 0.03125, ((0, 16), (1, 16))),
    }


neg_big = -1e+30
adapter_scale = 2.0

def group_attend(operands):
    group_query, group_key, group_value = operands
    scores = jnp.dot(group_query, group_key, preferred_element_type=jnp.float32) * (1.0 / math.sqrt(HEAD_SIZE))
    visible = jnp.arange(GROUP)[:, None] >= jnp.arange(GROUP)[None, :]
    masked = jnp.where(visible, scores, neg_big)
    row_max = lax.optimization_barrier(jnp.max(masked, axis=1, keepdims=True))
    weights = jnp.exp(masked - row_max)
    totals = lax.optimization_barrier(jnp.sum(weights, axis=1, keepdims=True))
    rounded = weights.astype(jnp.bfloat16)
    context = jnp.dot(rounded, group_value.T, preferred_element_type=jnp.float32) / totals
    return context.astype(jnp.bfloat16)

def one_head(head_index, queries, transposed_keys, transposed_values):
    pair_index = head_index // (H // KVH)
    head_query = lax.dynamic_slice_in_dim(queries, head_index * HEAD_SIZE, HEAD_SIZE, 1)
    head_key = lax.dynamic_slice_in_dim(transposed_keys, pair_index * HEAD_SIZE, HEAD_SIZE, 0)
    head_value = lax.dynamic_slice_in_dim(transposed_values, pair_index * HEAD_SIZE, HEAD_SIZE, 0)
    amount = jnp.where(head_index < H // 2, HALF, 0).astype(jnp.int32)
    head_query = jnp.roll(head_query, -amount, axis=0)
    head_key = jnp.roll(head_key, -amount, axis=1)
    head_value = jnp.roll(head_value, -amount, axis=1)
    group_count = SEQ_LEN // GROUP
    group_queries = head_query.reshape(group_count, GROUP, HEAD_SIZE)
    group_keys = jnp.transpose(head_key.reshape(HEAD_SIZE, group_count, GROUP), (1, 0, 2))
    group_values = jnp.transpose(head_value.reshape(HEAD_SIZE, group_count, GROUP), (1, 0, 2))
    context = lax.map(group_attend, (group_queries, group_keys, group_values))
    return jnp.roll(context.reshape(SEQ_LEN, HEAD_SIZE), amount, axis=0)

def reference(queries, transposed_keys, transposed_values, adapter_down_factor, adapter_up_factor, projection_output_gradient):

    def per_head(head_index):
        return one_head(head_index, queries, transposed_keys, transposed_values)
    contexts = lax.map(per_head, jnp.arange(H, dtype=jnp.int32))
    attention_result = jnp.transpose(contexts, (1, 0, 2)).reshape(SEQ_LEN, MODEL_WIDTH)
    adapter_activations = lax.dot_general(adapter_down_factor, attention_result, (((0,), (1,)), ((), ())), preferred_element_type=jnp.float32)
    rank_gradient_rows = lax.dot_general(adapter_up_factor, projection_output_gradient, (((1,), (1,)), ((), ())), preferred_element_type=jnp.float32).astype(jnp.bfloat16)
    down_factor_gradient = adapter_scale * lax.dot_general(attention_result, rank_gradient_rows, (((0,), (1,)), ((), ())), preferred_element_type=jnp.float32)
    rounded_activations = adapter_activations.astype(jnp.bfloat16)
    up_factor_gradient = adapter_scale * jnp.dot(rounded_activations, projection_output_gradient, preferred_element_type=jnp.float32)
    return (adapter_activations, down_factor_gradient, up_factor_gradient)
```

```python
import math

import jax
import jax.numpy as jnp
from jax import lax
from jax.experimental import pallas as pl
from jax.experimental.pallas import tpu as pltpu
from jax.sharding import Mesh, PartitionSpec as P

bf16 = jnp.bfloat16
f32 = jnp.float32
neg_big = -1e30
adapter_scale = 2.0
TILE = 256


def dot(a, b, dims=((1,), (0,))):
    return lax.dot_general(a, b, (dims, ((), ())), preferred_element_type=f32)


def load_keys(dst, own, other, core, half_dim):
    dst[pl.ds(pl.multiple_of(core * half_dim, half_dim), half_dim), :] = own
    dst[pl.ds(pl.multiple_of((1 - core) * half_dim, half_dim), half_dim), :] = other


def softmax_rows(scores, factor):
    top = jnp.max(scores, axis=1, keepdims=True)
    return top, jnp.exp2((scores - top) * factor).astype(bf16)


def diagonal_kernel(
    info, q_ref, ko_ref, kx_ref, vo_ref, vx_ref, down_ref,
    plain_ref, act_ref, part_ref, stat_ref, keys, values, turn,
):
    phase, head = pl.program_id(0), pl.program_id(1)
    shifted, core = info[0], info[1]
    half = jnp.where(phase == 0, shifted, 1 - shifted)
    length, head_dim = q_ref.shape
    half_dim = ko_ref.shape[0]
    factor = math.log2(math.e) / math.sqrt(head_dim)

    @pl.when((phase == 0) & (head == 0))
    def _():
        for part in range(2):
            cols = slice(part * length, (part + 1) * length)
            load_keys(keys.at[part], ko_ref[:, cols], kx_ref[:, cols], core, half_dim)
            load_keys(turn, vo_ref[:, cols], vx_ref[:, cols], core, half_dim)
            values[part, :, :head_dim] = turn[...].T
            values[part, :, head_dim:] = jnp.ones((length, head_dim), bf16)

    def rows_of(start):
        stop = start + TILE
        scores = dot(q_ref[start:stop, :], keys[half, :, :stop])
        row = lax.broadcasted_iota(jnp.int32, (TILE, TILE), 0)
        col = lax.broadcasted_iota(jnp.int32, (TILE, TILE), 1)
        last = jnp.where(row >= col, scores[:, start:], neg_big)
        scores = jnp.concatenate([scores[:, :start], last], axis=1) if start else last
        top, weights = softmax_rows(scores, factor)
        return top, dot(weights, values[half, :stop, :])

    @pl.when(phase == 0)
    def _():
        for start in range(0, length, TILE):
            _, out = rows_of(start)
            context = (out[:, :head_dim] / out[:, head_dim:]).astype(bf16)
            plain_ref[start : start + TILE, :] = context
            new = dot(down_ref[...], context, ((1,), (1,)))
            cols = slice(start, start + TILE)

            @pl.when(head == 0)
            def _():
                act_ref[:, cols] = new

            @pl.when(head != 0)
            def _():
                act_ref[:, cols] += new

    @pl.when(phase == 1)
    def _():
        for start in range(0, length, TILE):
            top, out = rows_of(start)
            rows = slice(start, start + TILE)
            part_ref[rows, :] = out[:, :head_dim]
            lane = lax.broadcasted_iota(jnp.int32, (TILE, head_dim), 1)
            old = stat_ref[rows, :]
            old = jnp.where(lane == head, top, old)
            stat_ref[rows, :] = jnp.where(lane == head + 8, out[:, head_dim:], old)


def cross_kernel(
    info, q_ref, ko_ref, kx_ref, vo_ref, vx_ref, ho_ref, hx_ref, part_ref, stat_ref,
    down_ref, plain_act_ref, back_ref, cross_ref, send_ref, keep_ref, keys, values, turn, act,
):
    head = pl.program_id(0)
    shifted, core = info[0], info[1]
    length, head_dim = q_ref.shape
    half_dim = ko_ref.shape[0]
    rank = down_ref.shape[0]
    factor = math.log2(math.e) / math.sqrt(head_dim)
    halo = shifted == 1

    @pl.when(head == 0)
    def _():
        load_keys(
            keys,
            jnp.where(halo, ho_ref[:half_dim, :], ko_ref[...]),
            jnp.where(halo, hx_ref[:half_dim, :], kx_ref[...]),
            core, half_dim,
        )
        load_keys(
            turn,
            jnp.where(halo, ho_ref[half_dim:, :], vo_ref[...]),
            jnp.where(halo, hx_ref[half_dim:, :], vx_ref[...]),
            core, half_dim,
        )
        values[:, :head_dim] = turn[...].T
        values[:, head_dim:] = jnp.ones((length, head_dim), bf16)
        act[...] = jnp.zeros_like(act)

    for start in range(0, length, TILE):
        rows = slice(start, start + TILE)
        scores = dot(q_ref[rows, :], keys[...])
        lane = lax.broadcasted_iota(jnp.int32, (TILE, head_dim), 1)
        stat = stat_ref[rows, :]
        top0 = jnp.sum(jnp.where(lane == head, stat, 0.0), axis=1, keepdims=True)
        sum0 = jnp.sum(jnp.where(lane == head + 8, stat, 0.0), axis=1, keepdims=True)
        top = jnp.maximum(jnp.max(scores, axis=1, keepdims=True), top0)
        weights = jnp.exp2((scores - top) * factor).astype(bf16)
        out = dot(weights, values[...])
        fade = jnp.exp2((top0 - top) * factor)
        total = out[:, head_dim:] + fade * sum0
        context = ((out[:, :head_dim] + fade * part_ref[rows, :]) / total).astype(bf16)
        cross_ref[rows, :] = context
        act[:, rows] += dot(down_ref[...], context, ((1,), (1,)))

    @pl.when(head == pl.num_programs(0) - 1)
    def _():
        same = shifted == core
        plain, cross = plain_act_ref[...], act[...]
        keep_ref[:rank, :] = jnp.where(same, plain, cross)
        send_ref[:rank, :] = jnp.where(same, cross, plain).astype(bf16)
        early, late = back_ref[:, :length], back_ref[:, length:]
        keep_ref[rank:, :] = jnp.where(core == 0, early, late)
        send_ref[rank:, :] = jnp.where(core == 0, late, early).astype(bf16)


def pair_sum_kernel(keep_ref, got_ref, out_ref):
    count, _, width = out_ref.shape
    for j in range(count):
        cols = slice(j * width, (j + 1) * width)
        out_ref[j] = (keep_ref[:, cols] + got_ref[:, cols].astype(f32)).astype(bf16)


def spread_sum_kernel(in_ref, out_ref, *, scale):
    count = in_ref.shape[0]
    total = in_ref[0].astype(f32)
    for j in range(1, count):
        total = total + in_ref[j].astype(f32)
    total = (total * scale).astype(out_ref.dtype)
    for j in range(count):
        out_ref[j] = total


def gradient_kernel(
    info, own_ref, other_ref, grad_ref, plain_ref, cross_ref, act_ref, out_ref, low, back
):
    shifted, core = info[0], info[1]
    count, rows, width = own_ref.shape
    rank = rows // 2
    length = count * width
    for j in range(count):
        a, b = own_ref[j], other_ref[j]
        early = jnp.where(core == 0, a, b)
        late = jnp.where(core == 0, b, a)
        for part, piece in enumerate((early, late)):
            cols = slice(part * length + j * width, part * length + (j + 1) * width)
            act_ref[:, cols] = piece[:rank].astype(f32)
            low[:, cols] = piece[:rank]
        swap = shifted == 1
        cols = slice(j * width, (j + 1) * width)
        back[0, :, cols] = jnp.where(swap, late, early)[rank:]
        back[1, :, cols] = jnp.where(swap, early, late)[rank:]
    out_ref[:rank, :] = dot(low[...], grad_ref[...])
    out_ref[rank:, :] = dot(back[0], plain_ref[...]) + dot(back[1], cross_ref[...])


def call(kernel, out_shape, **kw):
    return pl.pallas_call(kernel, out_shape=out_shape, **kw)


def shape(dims, dtype):
    return jax.ShapeDtypeStruct(dims, dtype)


def on_device(queries, keys, values, down, up, grad):
    core = lax.axis_index("core")
    zs = lax.axis_size("z")
    shifted = (lax.axis_index("z") < zs // 2).astype(jnp.int32)
    info = jnp.stack([shifted, core.astype(jnp.int32)])
    seq = lax.axis_size("seq")
    length, width = queries.shape
    half = length // 2
    half_dim = keys.shape[0]
    head_dim = 2 * half_dim
    heads = width // head_dim
    rank = up.shape[0]

    def to_partner(x):
        return lax.ppermute(x, "core", [(0, 1), (1, 0)])

    halo = jnp.concatenate([keys[:, half:], values[:, half:]], axis=0)
    halo = lax.ppermute(halo, "seq", [(i, (i + 1) % seq) for i in range(seq)])
    keys_other = to_partner(keys)
    values_other = to_partner(values)
    back_part = dot(up, grad, ((1,), (1,)))
    down_t = down.T

    whole = lambda *dims: pl.BlockSpec(dims, lambda *_: (0,) * len(dims))
    attend_params = pltpu.CompilerParams(vmem_limit_bytes=56 << 20)
    diag_cost = pl.CostEstimate(
        flops=4 * heads * half * half * head_dim, bytes_accessed=6 << 20,
        transcendentals=heads * half * half,
    )
    plain, act_plain, part, stat = pl.pallas_call(
        diagonal_kernel,
        grid_spec=pltpu.PrefetchScalarGridSpec(
            num_scalar_prefetch=1,
            grid=(2, heads),
            in_specs=[
                pl.BlockSpec(
                    (half, head_dim),
                    lambda g, h, s: (jnp.where(g == 0, s[0], 1 - s[0]), h),
                ),
                whole(half_dim, length), whole(half_dim, length),
                whole(half_dim, length), whole(half_dim, length),
                pl.BlockSpec((rank, head_dim), lambda g, h, s: (0, h)),
            ],
            out_specs=[
                pl.BlockSpec((half, head_dim), lambda g, h, s: (0, jnp.where(g == 0, h, heads - 1))),
                whole(rank, half),
                pl.BlockSpec((half, head_dim), lambda g, h, s: (0, jnp.where(g == 0, 0, h))),
                whole(half, head_dim),
            ],
            scratch_shapes=[
                pltpu.VMEM((2, head_dim, half), bf16),
                pltpu.VMEM((2, half, 2 * head_dim), bf16),
                pltpu.VMEM((head_dim, half), bf16),
            ],
        ),
        out_shape=[
            shape((half, width), bf16), shape((rank, half), f32),
            shape((half, width), f32), shape((half, head_dim), f32),
        ],
        compiler_params=attend_params,
        cost_estimate=diag_cost,
        name="diagonal",
    )(info, queries, keys, keys_other, values, values_other, down_t)

    halo_other = to_partner(halo)
    early = pl.BlockSpec((half_dim, half), lambda h, s: (0, 0))
    cross, send, keep = pl.pallas_call(
        cross_kernel,
        grid_spec=pltpu.PrefetchScalarGridSpec(
            num_scalar_prefetch=1,
            grid=(heads,),
            in_specs=[
                pl.BlockSpec((half, head_dim), lambda h, s: (1 - s[0], h)),
                early, early, early, early,
                whole(head_dim, half), whole(head_dim, half),
                pl.BlockSpec((half, head_dim), lambda h, s: (0, h)),
                whole(half, head_dim),
                pl.BlockSpec((rank, head_dim), lambda h, s: (0, h)),
                whole(rank, half), whole(rank, length),
            ],
            out_specs=[
                pl.BlockSpec((half, head_dim), lambda h, s: (0, h)),
                whole(2 * rank, half), whole(2 * rank, half),
            ],
            scratch_shapes=[
                pltpu.VMEM((head_dim, half), bf16),
                pltpu.VMEM((half, 2 * head_dim), bf16),
                pltpu.VMEM((head_dim, half), bf16),
                pltpu.VMEM((rank, half), f32),
            ],
        ),
        out_shape=[
            shape((half, width), bf16), shape((2 * rank, half), bf16), shape((2 * rank, half), f32),
        ],
        compiler_params=attend_params,
        cost_estimate=pl.CostEstimate(
            flops=4 * heads * half * half * head_dim, bytes_accessed=6 << 20,
            transcendentals=heads * half * half,
        ),
        name="cross",
    )(info, queries, keys, keys_other, values, values_other, halo, halo_other, part, stat,
      down_t, act_plain, back_part)

    got = to_partner(send)
    chunk = half // zs
    sent = call(pair_sum_kernel, shape((zs, 2 * rank, chunk), bf16), name="pair_sum")(keep, got)
    terms = lax.all_to_all(sent, "z", 0, 0)
    spread = call(
        lambda a, b: spread_sum_kernel(a, b, scale=1.0),
        shape((zs, 2 * rank, chunk), bf16), name="z_sum",
    )(terms)
    own = lax.all_to_all(spread, "z", 0, 0)
    other = to_partner(own)
    smem = pl.BlockSpec(memory_space=pltpu.SMEM)
    vmem = pl.BlockSpec(memory_space=pltpu.VMEM)
    activations, factors = call(
        gradient_kernel, [shape((rank, length), f32), shape((2 * rank, width), f32)],
        in_specs=[smem] + [vmem] * 5, out_specs=[vmem, vmem],
        scratch_shapes=[pltpu.VMEM((rank, length), bf16), pltpu.VMEM((2, rank, half), bf16)],
        compiler_params=pltpu.CompilerParams(vmem_limit_bytes=40 << 20),
        name="gradients",
    )(info, own, other, grad, plain, cross)
    pieces = factors.reshape(seq, 2 * rank // seq, width)
    terms = lax.all_to_all(pieces, "seq", 0, 0)
    spread = call(
        lambda a, b: spread_sum_kernel(a, b, scale=adapter_scale),
        shape(pieces.shape, f32), name="seq_sum",
    )(terms)
    done = lax.all_to_all(spread, "seq", 0, 0).reshape(2 * rank, width)
    return activations, done[rank:].T, done[:rank]


def solution(mesh):
    devices = mesh.devices
    split = Mesh(devices.reshape(devices.shape[0], devices.shape[1] // 2, 2), ("seq", "z", "core"))
    head = ("z", "core")
    in_specs = (
        P("seq", head),
        P(head, "seq"),
        P(head, "seq"),
        P(head, None),
        P(None, head),
        P("seq", head),
    )
    out_specs = (P(None, "seq"), P(head, None), P(None, head))
    return jax.shard_map(
        on_device, mesh=split, in_specs=in_specs, out_specs=out_specs, check_vma=False
    )
```

```python
import math

import jax
import jax.numpy as jnp
from jax import lax
from jax.experimental import pallas as pl
from jax.experimental.pallas import tpu as pltpu
from jax.sharding import Mesh, PartitionSpec as P

bf16 = jnp.bfloat16
f32 = jnp.float32
neg_big = -1e30
adapter_scale = 2.0
TILE = 256


def dot(a, b, dims=((1,), (0,))):
    return lax.dot_general(a, b, (dims, ((), ())), preferred_element_type=f32)


def load_keys(dst, own, other, core, half_dim):
    dst[pl.ds(pl.multiple_of(core * half_dim, half_dim), half_dim), :] = own
    dst[pl.ds(pl.multiple_of((1 - core) * half_dim, half_dim), half_dim), :] = other


def load_values(dst, turn, head_dim):
    dst[:, :head_dim] = turn[...].T
    dst[:, head_dim:] = jnp.ones((dst.shape[0], dst.shape[1] - head_dim), bf16)


def pipeline(tiles, score, weigh, finish):
    tops, ready = {}, {}
    for step in range(len(tiles) + 2):
        if step < len(tiles):
            tops[step] = score(tiles[step], step % 2)
        if 1 <= step <= len(tiles):
            ready[step - 1] = weigh(tiles[step - 1], tops.pop(step - 1), (step - 1) % 2)
        if 2 <= step:
            finish(tiles[step - 2], ready.pop(step - 2), (step - 2) % 2)


def diagonal_kernel(
    info, q_ref, ko_ref, kx_ref, vo_ref, vx_ref, down_ref,
    plain_ref, act_ref, part_ref, stat_ref,
    keys, values, turn, s0, s1, p0, p1,
):
    shifted, core = info[0], info[1]
    half_dim = ko_ref.shape[0]
    head_dim = 2 * half_dim
    length = q_ref.shape[0] // 2
    heads = q_ref.shape[1] // head_dim
    factor = math.log2(math.e) / math.sqrt(head_dim)
    score_bufs, weight_bufs = (s0, s1), (p0, p1)
    for part in range(2):
        cols = slice(part * length, (part + 1) * length)
        load_keys(keys.at[part], ko_ref[:, cols], kx_ref[:, cols], core, half_dim)
        load_keys(turn, vo_ref[:, cols], vx_ref[:, cols], core, half_dim)
        load_values(values.at[part], turn, head_dim)
    halves = (shifted, 1 - shifted)

    def score(tile, slot):
        phase, head, start = tile
        stop = start + TILE
        base = pl.multiple_of(halves[phase] * length + start, TILE)
        query = q_ref[pl.ds(base, TILE), head * head_dim : (head + 1) * head_dim]
        scores = dot(query, keys[halves[phase], :, :stop])
        row = lax.broadcasted_iota(jnp.int32, (TILE, TILE), 0)
        col = lax.broadcasted_iota(jnp.int32, (TILE, TILE), 1)
        last = jnp.where(row >= col, scores[:, start:], neg_big)
        top = jnp.max(last, axis=1, keepdims=True)
        score_bufs[slot][:, start:stop] = last
        if start:
            top = jnp.maximum(top, jnp.max(scores[:, :start], axis=1, keepdims=True))
            score_bufs[slot][:, :start] = scores[:, :start]
        return top

    def weigh(tile, top, slot):
        phase, head, start = tile
        stop = start + TILE
        weight_bufs[slot][:, :stop] = jnp.exp2((score_bufs[slot][:, :stop] - top) * factor).astype(bf16)
        return top

    def finish(tile, top, slot):
        phase, head, start = tile
        stop = start + TILE
        rows, cols = slice(start, stop), slice(head * head_dim, (head + 1) * head_dim)
        out = dot(weight_bufs[slot][:, :stop], values[halves[phase], :stop, :])
        if phase == 0:
            plain_ref[rows, cols] = (out[:, :head_dim] / out[:, head_dim:]).astype(bf16)
        else:
            part_ref[rows, cols] = out[:, :head_dim]
            stat_ref[rows, head : head + 1] = top
            stat_ref[rows, heads + head : heads + head + 1] = out[:, head_dim : head_dim + 1]

    tiles = [
        (phase, head, start)
        for phase in range(2) for head in range(heads) for start in range(0, length, TILE)
    ]
    pipeline(tiles, score, weigh, finish)
    act_ref[...] = dot(down_ref[...], plain_ref[...], ((1,), (1,)))


def cross_kernel(
    info, q_ref, ko_ref, kx_ref, vo_ref, vx_ref, ho_ref, hx_ref, part_ref, stat_ref,
    down_ref, plain_act_ref, back_ref, cross_ref, send_ref, keep_ref,
    keys, values, turn, s0, s1, p0, p1,
):
    shifted, core = info[0], info[1]
    half_dim = ko_ref.shape[0]
    head_dim = 2 * half_dim
    length = q_ref.shape[0] // 2
    heads = q_ref.shape[1] // head_dim
    rank = down_ref.shape[0]
    factor = math.log2(math.e) / math.sqrt(head_dim)
    score_bufs, weight_bufs = (s0, s1), (p0, p1)
    halo = shifted == 1
    load_keys(
        keys,
        jnp.where(halo, ho_ref[:half_dim, :], ko_ref[:, :length]),
        jnp.where(halo, hx_ref[:half_dim, :], kx_ref[:, :length]),
        core, half_dim,
    )
    load_keys(
        turn,
        jnp.where(halo, ho_ref[half_dim:, :], vo_ref[:, :length]),
        jnp.where(halo, hx_ref[half_dim:, :], vx_ref[:, :length]),
        core, half_dim,
    )
    load_values(values, turn, head_dim)

    def score(tile, slot):
        head, start = tile
        base = pl.multiple_of((1 - shifted) * length + start, TILE)
        query = q_ref[pl.ds(base, TILE), head * head_dim : (head + 1) * head_dim]
        scores = dot(query, keys[...])
        score_bufs[slot][...] = scores
        top = jnp.max(scores, axis=1, keepdims=True)
        return jnp.maximum(top, stat_ref[start : start + TILE, head : head + 1])

    def weigh(tile, top, slot):
        weight_bufs[slot][...] = jnp.exp2((score_bufs[slot][...] - top) * factor).astype(bf16)
        return top

    def finish(tile, top, slot):
        head, start = tile
        rows, cols = slice(start, start + TILE), slice(head * head_dim, (head + 1) * head_dim)
        out = dot(weight_bufs[slot][...], values[...])
        fade = jnp.exp2((stat_ref[rows, head : head + 1] - top) * factor)
        total = out[:, head_dim:] + fade * stat_ref[rows, heads + head : heads + head + 1]
        cross_ref[rows, cols] = (
            (out[:, :head_dim] + fade * part_ref[rows, cols]) / total
        ).astype(bf16)

    pipeline(
        [(head, start) for head in range(heads) for start in range(0, length, TILE)],
        score, weigh, finish,
    )
    cross = dot(down_ref[...], cross_ref[...], ((1,), (1,)))
    same = shifted == core
    plain = plain_act_ref[...]
    keep_ref[:rank, :] = jnp.where(same, plain, cross)
    send_ref[:rank, :] = jnp.where(same, cross, plain).astype(bf16)
    early, late = back_ref[:, :length], back_ref[:, length:]
    keep_ref[rank:, :] = jnp.where(core == 0, early, late)
    send_ref[rank:, :] = jnp.where(core == 0, late, early).astype(bf16)


def halo_kernel(k_ref, v_ref, out_ref):
    rows, length = k_ref.shape[0], out_ref.shape[1]
    out_ref[:rows, :] = k_ref[:, length:]
    out_ref[rows:, :] = v_ref[:, length:]


def pair_sum_kernel(keep_ref, got_ref, out_ref):
    count, _, width = out_ref.shape
    for j in range(count):
        cols = slice(j * width, (j + 1) * width)
        out_ref[j] = (keep_ref[:, cols] + got_ref[:, cols].astype(f32)).astype(bf16)


def spread_sum_kernel(in_ref, out_ref, *, scale):
    count = in_ref.shape[0]
    total = in_ref[0].astype(f32)
    for j in range(1, count):
        total = total + in_ref[j].astype(f32)
    total = (total * scale).astype(out_ref.dtype)
    for j in range(count):
        out_ref[j] = total


def gradient_kernel(
    info, own_ref, other_ref, grad_ref, plain_ref, cross_ref, act_ref, out_ref, low, back
):
    shifted, core = info[0], info[1]
    count, rows, width = own_ref.shape
    rank = rows // 2
    length = count * width
    for j in range(count):
        a, b = own_ref[j], other_ref[j]
        early = jnp.where(core == 0, a, b)
        late = jnp.where(core == 0, b, a)
        for part, piece in enumerate((early, late)):
            cols = slice(part * length + j * width, part * length + (j + 1) * width)
            act_ref[:, cols] = piece[:rank].astype(f32)
            low[:, cols] = piece[:rank]
        swap = shifted == 1
        cols = slice(j * width, (j + 1) * width)
        back[0, :, cols] = jnp.where(swap, late, early)[rank:]
        back[1, :, cols] = jnp.where(swap, early, late)[rank:]
    out_ref[:rank, :] = dot(low[...], grad_ref[...])
    out_ref[rank:, :] = dot(back[0], plain_ref[...]) + dot(back[1], cross_ref[...])


def call(kernel, out_shape, operands, name, scalars=0, scratch=(), cost=None, limit=24):
    smem = pl.BlockSpec(memory_space=pltpu.SMEM)
    vmem = pl.BlockSpec(memory_space=pltpu.VMEM)
    return pl.pallas_call(
        kernel,
        out_shape=out_shape,
        in_specs=[smem] * scalars + [vmem] * (len(operands) - scalars),
        out_specs=[vmem] * len(out_shape) if isinstance(out_shape, list) else vmem,
        scratch_shapes=scratch,
        compiler_params=pltpu.CompilerParams(vmem_limit_bytes=limit << 20),
        cost_estimate=cost,
        name=name,
    )(*operands)


def shape(dims, dtype):
    return jax.ShapeDtypeStruct(dims, dtype)


def on_device(queries, keys, values, down, up, grad):
    core = lax.axis_index("core")
    zs = lax.axis_size("z")
    shifted = (lax.axis_index("z") < zs // 2).astype(jnp.int32)
    info = jnp.stack([shifted, core.astype(jnp.int32)])
    seq = lax.axis_size("seq")
    length, width = queries.shape
    half = length // 2
    half_dim = keys.shape[0]
    head_dim = 2 * half_dim
    heads = width // head_dim
    rank = up.shape[0]

    def to_partner(x):
        return lax.ppermute(x, "core", [(0, 1), (1, 0)])

    keys_other = to_partner(keys)
    values_other = to_partner(values)
    later = call(halo_kernel, shape((head_dim, half), bf16), (keys, values), "halo", limit=8)
    halo = lax.ppermute(later, "seq", [(i, (i + 1) % seq) for i in range(seq)])
    halo_other = lax.ppermute(
        later, ("seq", "core"),
        [(2 * i + c, (2 * i + 2) % (2 * seq) + 1 - c) for i in range(seq) for c in range(2)],
    )
    back_part = dot(up, grad, ((1,), (1,)))
    down_t = down.T

    tile_scratch = [
        pltpu.VMEM((TILE, half), f32), pltpu.VMEM((TILE, half), f32),
        pltpu.VMEM((TILE, half), bf16), pltpu.VMEM((TILE, half), bf16),
    ]
    cost = pl.CostEstimate(
        flops=4 * heads * half * half * head_dim, bytes_accessed=6 << 20,
        transcendentals=heads * half * half,
    )
    plain, act_plain, part, stat = call(
        diagonal_kernel,
        [
            shape((half, width), bf16), shape((rank, half), f32),
            shape((half, width), f32), shape((half, 2 * heads), f32),
        ],
        (info, queries, keys, keys_other, values, values_other, down_t),
        "diagonal", scalars=1, cost=cost,
        scratch=[
            pltpu.VMEM((2, head_dim, half), bf16),
            pltpu.VMEM((2, half, 2 * head_dim), bf16),
            pltpu.VMEM((head_dim, half), bf16),
        ] + tile_scratch,
    )
    cross, send, keep = call(
        cross_kernel,
        [shape((half, width), bf16), shape((2 * rank, half), bf16), shape((2 * rank, half), f32)],
        (info, queries, keys, keys_other, values, values_other, halo, halo_other, part, stat,
         down_t, act_plain, back_part),
        "cross", scalars=1, cost=cost,
        scratch=[
            pltpu.VMEM((head_dim, half), bf16),
            pltpu.VMEM((half, 2 * head_dim), bf16),
            pltpu.VMEM((head_dim, half), bf16),
        ] + tile_scratch,
    )

    got = to_partner(send)
    chunk = half // zs
    sent = call(pair_sum_kernel, shape((zs, 2 * rank, chunk), bf16), (keep, got), "pair_sum", limit=8)
    terms = lax.all_to_all(sent, "z", 0, 0)
    spread = call(
        lambda a, b: spread_sum_kernel(a, b, scale=1.0),
        shape((zs, 2 * rank, chunk), bf16), (terms,), "z_sum", limit=8,
    )
    own = lax.all_to_all(spread, "z", 0, 0)
    other = to_partner(own)
    activations, factors = call(
        gradient_kernel, [shape((rank, length), f32), shape((2 * rank, width), f32)],
        (info, own, other, grad, plain, cross), "gradients", scalars=1,
        scratch=[pltpu.VMEM((rank, length), bf16), pltpu.VMEM((2, rank, half), bf16)],
    )
    pieces = factors.reshape(seq, 2 * rank // seq, width)
    terms = lax.all_to_all(pieces, "seq", 0, 0)
    spread = call(
        lambda a, b: spread_sum_kernel(a, b, scale=adapter_scale),
        shape(pieces.shape, f32), (terms,), "seq_sum", limit=8,
    )
    done = lax.all_to_all(spread, "seq", 0, 0).reshape(2 * rank, width)
    return activations, done[rank:].T, done[:rank]


def solution(mesh):
    devices = mesh.devices
    split = Mesh(devices.reshape(devices.shape[0], devices.shape[1] // 2, 2), ("seq", "z", "core"))
    head = ("z", "core")
    in_specs = (
        P("seq", head),
        P(head, "seq"),
        P(head, "seq"),
        P(head, None),
        P(None, head),
        P("seq", head),
    )
    out_specs = (P(None, "seq"), P(head, None), P(None, head))
    return jax.shard_map(
        on_device, mesh=split, in_specs=in_specs, out_specs=out_specs, check_vma=False
    )
```

```python
import functools
import math

import jax
import jax.numpy as jnp
from jax import lax
from jax.experimental import pallas as pl
from jax.experimental.pallas import tpu as pltpu
from jax.sharding import Mesh, PartitionSpec as P

bf16 = jnp.bfloat16
f32 = jnp.float32
neg_big = -1e30
adapter_scale = 2.0
TILE = 256


def dot(a, b, dims=((1,), (0,))):
    return lax.dot_general(a, b, (dims, ((), ())), preferred_element_type=f32)


def load_keys(dst, own, other, core, half_dim):
    dst[pl.ds(pl.multiple_of(core * half_dim, half_dim), half_dim), :] = own
    dst[pl.ds(pl.multiple_of((1 - core) * half_dim, half_dim), half_dim), :] = other


def load_values(dst, turn, head_dim):
    dst[:, :head_dim] = turn[...].T
    dst[:, head_dim:] = jnp.ones((dst.shape[0], dst.shape[1] - head_dim), bf16)


def pipeline(tiles, score, weigh, finish):
    tops, ready = {}, {}
    for step in range(len(tiles) + 2):
        if step < len(tiles):
            tops[step] = score(tiles[step], step % 2)
        if 1 <= step <= len(tiles):
            ready[step - 1] = weigh(tiles[step - 1], tops.pop(step - 1), (step - 1) % 2)
        if 2 <= step:
            finish(tiles[step - 2], ready.pop(step - 2), (step - 2) % 2)


def diagonal_kernel(
    info, q_ref, ko_ref, kx_ref, vo_ref, vx_ref, down_ref,
    plain_ref, act_ref, part_ref, stat_ref,
    keys, values, turn, s0, s1, p0, p1,
):
    shifted, core = info[0], info[1]
    half_dim = ko_ref.shape[0]
    head_dim = 2 * half_dim
    length = q_ref.shape[0] // 2
    heads = q_ref.shape[1] // head_dim
    factor = math.log2(math.e) / math.sqrt(head_dim)
    score_bufs, weight_bufs = (s0, s1), (p0, p1)
    for part in range(2):
        cols = slice(part * length, (part + 1) * length)
        load_keys(keys.at[part], ko_ref[:, cols], kx_ref[:, cols], core, half_dim)
        load_keys(turn, vo_ref[:, cols], vx_ref[:, cols], core, half_dim)
        load_values(values.at[part], turn, head_dim)
    halves = (shifted, 1 - shifted)

    def score(tile, slot):
        phase, head, start = tile
        stop = start + TILE
        base = pl.multiple_of(halves[phase] * length + start, TILE)
        query = q_ref[pl.ds(base, TILE), head * head_dim : (head + 1) * head_dim]
        scores = dot(query, keys[halves[phase], :, :stop])
        row = lax.broadcasted_iota(jnp.int32, (TILE, TILE), 0)
        col = lax.broadcasted_iota(jnp.int32, (TILE, TILE), 1)
        last = jnp.where(row >= col, scores[:, start:], neg_big)
        top = jnp.max(last, axis=1, keepdims=True)
        score_bufs[slot][:, start:stop] = last
        if start:
            top = jnp.maximum(top, jnp.max(scores[:, :start], axis=1, keepdims=True))
            score_bufs[slot][:, :start] = scores[:, :start]
        return top

    def weigh(tile, top, slot):
        phase, head, start = tile
        stop = start + TILE
        weight_bufs[slot][:, :stop] = jnp.exp2((score_bufs[slot][:, :stop] - top) * factor).astype(bf16)
        return top

    def finish(tile, top, slot):
        phase, head, start = tile
        stop = start + TILE
        rows, cols = slice(start, stop), slice(head * head_dim, (head + 1) * head_dim)
        out = dot(weight_bufs[slot][:, :stop], values[halves[phase], :stop, :])
        if phase == 0:
            plain_ref[rows, cols] = (out[:, :head_dim] / out[:, head_dim:]).astype(bf16)
        else:
            part_ref[rows, cols] = out[:, :head_dim]
            stat_ref[rows, head : head + 1] = top
            stat_ref[rows, heads + head : heads + head + 1] = out[:, head_dim : head_dim + 1]

    tiles = [
        (phase, head, start)
        for phase in range(2) for head in range(heads) for start in range(0, length, TILE)
    ]
    pipeline(tiles, score, weigh, finish)
    act_ref[...] = dot(down_ref[...], plain_ref[...], ((1,), (1,)))


def cross_kernel(
    info, q_ref, ko_ref, kx_ref, vo_ref, vx_ref, ho_ref, hx_ref, part_ref, stat_ref,
    down_ref, plain_act_ref, back_ref, cross_ref, send_ref, keep_ref,
    keys, values, turn, s0, s1, p0, p1,
):
    shifted, core = info[0], info[1]
    half_dim = ko_ref.shape[0]
    head_dim = 2 * half_dim
    length = q_ref.shape[0] // 2
    heads = q_ref.shape[1] // head_dim
    rank = down_ref.shape[0]
    factor = math.log2(math.e) / math.sqrt(head_dim)
    score_bufs, weight_bufs = (s0, s1), (p0, p1)
    halo = shifted == 1
    load_keys(
        keys,
        jnp.where(halo, ho_ref[:half_dim, :], ko_ref[:, :length]),
        jnp.where(halo, hx_ref[:half_dim, :], kx_ref[:, :length]),
        core, half_dim,
    )
    load_keys(
        turn,
        jnp.where(halo, ho_ref[half_dim:, :], vo_ref[:, :length]),
        jnp.where(halo, hx_ref[half_dim:, :], vx_ref[:, :length]),
        core, half_dim,
    )
    load_values(values, turn, head_dim)

    def score(tile, slot):
        head, start = tile
        base = pl.multiple_of((1 - shifted) * length + start, TILE)
        query = q_ref[pl.ds(base, TILE), head * head_dim : (head + 1) * head_dim]
        scores = dot(query, keys[...])
        score_bufs[slot][...] = scores
        top = jnp.max(scores, axis=1, keepdims=True)
        return jnp.maximum(top, stat_ref[start : start + TILE, head : head + 1])

    def weigh(tile, top, slot):
        weight_bufs[slot][...] = jnp.exp2((score_bufs[slot][...] - top) * factor).astype(bf16)
        return top

    def finish(tile, top, slot):
        head, start = tile
        rows, cols = slice(start, start + TILE), slice(head * head_dim, (head + 1) * head_dim)
        out = dot(weight_bufs[slot][...], values[...])
        fade = jnp.exp2((stat_ref[rows, head : head + 1] - top) * factor)
        total = out[:, head_dim:] + fade * stat_ref[rows, heads + head : heads + head + 1]
        cross_ref[rows, cols] = (
            (out[:, :head_dim] + fade * part_ref[rows, cols]) / total
        ).astype(bf16)

    pipeline(
        [(head, start) for head in range(heads) for start in range(0, length, TILE)],
        score, weigh, finish,
    )
    cross = dot(down_ref[...], cross_ref[...], ((1,), (1,)))
    same = shifted == core
    plain = plain_act_ref[...]
    keep_ref[:rank, :] = jnp.where(same, plain, cross)
    send_ref[:rank, :] = jnp.where(same, cross, plain).astype(bf16)
    early, late = back_ref[:, :length], back_ref[:, length:]
    keep_ref[rank:, :] = jnp.where(core == 0, early, late)
    send_ref[rank:, :] = jnp.where(core == 0, late, early).astype(bf16)


def stage_kernel(k_hbm, v_hbm, k_near, v_near, halo_ref, sems):
    rows, length = k_near.shape[0], halo_ref.shape[1]
    copies = [
        pltpu.make_async_copy(k_hbm, k_near, sems.at[0]),
        pltpu.make_async_copy(v_hbm, v_near, sems.at[1]),
    ]
    for copy in copies:
        copy.start()
    copies[0].wait()
    halo_ref[:rows, :] = k_near[:, length:]
    copies[1].wait()
    halo_ref[rows:, :] = v_near[:, length:]


def pair_sum_kernel(keep_ref, got_ref, out_ref):
    count, _, width = out_ref.shape
    for j in range(count):
        cols = slice(j * width, (j + 1) * width)
        out_ref[j] = (keep_ref[:, cols] + got_ref[:, cols].astype(f32)).astype(bf16)


def spread_sum_kernel(in_ref, out_ref, *, scale):
    count = in_ref.shape[0]
    total = in_ref[0].astype(f32)
    for j in range(1, count):
        total = total + in_ref[j].astype(f32)
    total = (total * scale).astype(out_ref.dtype)
    for j in range(count):
        out_ref[j] = total


def gradient_kernel(info, piece_ref, grad_ref, plain_ref, cross_ref, *rest, other):
    if other:
        act_before, before, act_hbm, out_ref, low, back, act, sems = rest
    else:
        act, out_ref, low, back = rest
    shifted, core = info[0], info[1]
    count, rows, width = piece_ref.shape
    rank = rows // 2
    length = count * width
    half = 1 - core if other else core
    own = pl.ds(pl.multiple_of(half * length, length), length)
    stores = []
    if other:
        early = pl.ds(pl.multiple_of(core * length, length), length)
        stores.append(pltpu.make_async_copy(act_before, act_hbm.at[:, early], sems.at[0]))
        stores[0].start()
    for j in range(count):
        piece = piece_ref[j]
        cols = slice(j * width, (j + 1) * width)
        low[:, cols] = piece[:rank]
        back[:, cols] = piece[rank:]
        act[:, cols] = piece[:rank].astype(f32)
    if other:
        stores.append(pltpu.make_async_copy(act, act_hbm.at[:, own], sems.at[1]))
        stores[1].start()
    attention = jnp.where(shifted == half, plain_ref[...], cross_ref[...])
    upper = dot(low[...], grad_ref[own, :])
    lower = dot(back[...], attention)
    out_ref[:rank, :] = before[:rank, :] + upper if other else upper
    out_ref[rank:, :] = before[rank:, :] + lower if other else lower
    for store in stores:
        store.wait()


def call(kernel, out_shape, operands, name, scalars=0, hbm=0, hbm_out=0, scratch=(), cost=None, limit=24):
    smem = pl.BlockSpec(memory_space=pltpu.SMEM)
    vmem = pl.BlockSpec(memory_space=pltpu.VMEM)
    far = pl.BlockSpec(memory_space=pltpu.HBM)
    return pl.pallas_call(
        kernel,
        out_shape=out_shape,
        in_specs=[smem] * scalars + [far] * hbm + [vmem] * (len(operands) - scalars - hbm),
        out_specs=[far] * hbm_out + [vmem] * (len(out_shape) - hbm_out)
        if isinstance(out_shape, list) else vmem,
        scratch_shapes=scratch,
        compiler_params=pltpu.CompilerParams(vmem_limit_bytes=limit << 20),
        cost_estimate=cost,
        name=name,
    )(*operands)


def shape(dims, dtype):
    return jax.ShapeDtypeStruct(dims, dtype)


def on_device(queries, keys, values, down, up, grad):
    core = lax.axis_index("core")
    zs = lax.axis_size("z")
    shifted = (lax.axis_index("z") < zs // 2).astype(jnp.int32)
    info = jnp.stack([shifted, core.astype(jnp.int32)])
    seq = lax.axis_size("seq")
    length, width = queries.shape
    half = length // 2
    half_dim = keys.shape[0]
    head_dim = 2 * half_dim
    heads = width // head_dim
    rank = up.shape[0]

    def to_partner(x):
        return lax.ppermute(x, "core", [(0, 1), (1, 0)])

    def far(x):
        return pltpu.with_memory_space_constraint(x, pltpu.HBM)

    keys, values, later = call(
        stage_kernel,
        [shape(keys.shape, bf16), shape(values.shape, bf16), shape((head_dim, half), bf16)],
        (far(keys), far(values)), "stage", hbm=2, limit=8,
        scratch=[pltpu.SemaphoreType.DMA((2,))],
        cost=pl.CostEstimate(flops=8 << 30, bytes_accessed=1 << 20, transcendentals=0),
    )
    keys_other = to_partner(keys)
    values_other = to_partner(values)
    halo = lax.ppermute(later, "seq", [(i, (i + 1) % seq) for i in range(seq)])
    down_t = down.T

    tile_scratch = [
        pltpu.VMEM((TILE, half), f32), pltpu.VMEM((TILE, half), f32),
        pltpu.VMEM((TILE, half), bf16), pltpu.VMEM((TILE, half), bf16),
    ]
    cost = pl.CostEstimate(
        flops=4 * heads * half * half * head_dim, bytes_accessed=6 << 20,
        transcendentals=heads * half * half,
    )
    plain, act_plain, part, stat = call(
        diagonal_kernel,
        [
            shape((half, width), bf16), shape((rank, half), f32),
            shape((half, width), f32), shape((half, 2 * heads), f32),
        ],
        (info, queries, keys, keys_other, values, values_other, down_t),
        "diagonal", scalars=1, cost=cost,
        scratch=[
            pltpu.VMEM((2, head_dim, half), bf16),
            pltpu.VMEM((2, half, 2 * head_dim), bf16),
            pltpu.VMEM((head_dim, half), bf16),
        ] + tile_scratch,
    )
    halo, up, act_plain = lax.optimization_barrier((halo, up, act_plain))
    halo_other = to_partner(halo)
    back_part = dot(up, grad, ((1,), (1,)))
    cross, send, keep = call(
        cross_kernel,
        [shape((half, width), bf16), shape((2 * rank, half), bf16), shape((2 * rank, half), f32)],
        (info, queries, keys, keys_other, values, values_other, halo, halo_other, part, stat,
         down_t, act_plain, back_part),
        "cross", scalars=1, cost=cost,
        scratch=[
            pltpu.VMEM((head_dim, half), bf16),
            pltpu.VMEM((half, 2 * head_dim), bf16),
            pltpu.VMEM((head_dim, half), bf16),
        ] + tile_scratch,
    )

    got = to_partner(send)
    chunk = half // zs
    sent = call(pair_sum_kernel, shape((zs, 2 * rank, chunk), bf16), (keep, got), "pair_sum", limit=8)
    terms = lax.all_to_all(sent, "z", 0, 0)
    spread = call(
        lambda a, b: spread_sum_kernel(a, b, scale=1.0),
        shape((zs, 2 * rank, chunk), bf16), (terms,), "z_sum", limit=8,
    )
    own = lax.all_to_all(spread, "z", 0, 0)
    other = to_partner(own)
    grads = ()
    for piece, columns, name in ((own, half, "gradients_own"), (other, length, "gradients_other")):
        grads = call(
            functools.partial(gradient_kernel, other=bool(grads)),
            [shape((rank, columns), f32), shape((2 * rank, width), f32)],
            (info, piece, grad, plain, cross, *grads),
            name, scalars=1, hbm_out=len(grads) // 2, limit=16,
            scratch=[pltpu.VMEM((rank, half), bf16), pltpu.VMEM((rank, half), bf16)]
            + ([pltpu.VMEM((rank, half), f32), pltpu.SemaphoreType.DMA((2,))] if grads else []),
            cost=pl.CostEstimate(
                flops=4 * rank * half * width, bytes_accessed=4 << 20, transcendentals=0
            ),
        )
    activations, factors = grads
    pieces = factors.reshape(seq, 2 * rank // seq, width)
    terms = lax.all_to_all(pieces, "seq", 0, 0)
    spread = call(
        lambda a, b: spread_sum_kernel(a, b, scale=adapter_scale),
        shape(pieces.shape, f32), (terms,), "seq_sum", limit=8,
    )
    done = lax.all_to_all(spread, "seq", 0, 0).reshape(2 * rank, width)
    return activations, done[rank:].T, done[:rank]


def solution(mesh):
    devices = mesh.devices
    split = Mesh(devices.reshape(devices.shape[0], devices.shape[1] // 2, 2), ("seq", "z", "core"))
    head = ("z", "core")
    in_specs = (
        P("seq", head),
        P(head, "seq"),
        P(head, "seq"),
        P(head, None),
        P(None, head),
        P("seq", head),
    )
    out_specs = (P(None, "seq"), P(head, None), P(None, head))
    return jax.shard_map(
        on_device, mesh=split, in_specs=in_specs, out_specs=out_specs, check_vma=False
    )
```

```python
import functools
import math

import jax
import jax.numpy as jnp
from jax import lax
from jax.experimental import pallas as pl
from jax.experimental.pallas import tpu as pltpu
from jax.sharding import Mesh, PartitionSpec as P

bf16 = jnp.bfloat16
f32 = jnp.float32
neg_big = -1e30
adapter_scale = 2.0
TILE = 256


def dot(a, b, dims=((1,), (0,))):
    return lax.dot_general(a, b, (dims, ((), ())), preferred_element_type=f32)


def load_keys(dst, own, other, core, half_dim):
    dst[pl.ds(pl.multiple_of(core * half_dim, half_dim), half_dim), :] = own
    dst[pl.ds(pl.multiple_of((1 - core) * half_dim, half_dim), half_dim), :] = other


def load_values(dst, turn, head_dim):
    dst[:, :head_dim] = turn[...].T
    dst[:, head_dim:] = jnp.ones((dst.shape[0], dst.shape[1] - head_dim), bf16)


def pipeline(tiles, score, weigh, finish):
    tops, ready = {}, {}
    for step in range(len(tiles) + 2):
        if step < len(tiles):
            tops[step] = score(tiles[step], step % 2)
        if 1 <= step <= len(tiles):
            ready[step - 1] = weigh(tiles[step - 1], tops.pop(step - 1), (step - 1) % 2)
        if 2 <= step:
            finish(tiles[step - 2], ready.pop(step - 2), (step - 2) % 2)


def diagonal_kernel(
    info, q_ref, own_ref, other_ref, down_ref,
    plain_ref, act_ref, part_ref, stat_ref,
    keys, values, turn, s0, s1, p0, p1,
):
    shifted, core = info[0], info[1]
    head_dim = own_ref.shape[0]
    half_dim = head_dim // 2
    length = q_ref.shape[0] // 2
    heads = q_ref.shape[1] // head_dim
    factor = math.log2(math.e) / math.sqrt(head_dim)
    score_bufs, weight_bufs = (s0, s1), (p0, p1)
    for part in range(2):
        cols = slice(part * length, (part + 1) * length)
        load_keys(keys.at[part], own_ref[:half_dim, cols], other_ref[:half_dim, cols], core, half_dim)
        load_keys(turn, own_ref[half_dim:, cols], other_ref[half_dim:, cols], core, half_dim)
        load_values(values.at[part], turn, head_dim)
    halves = (shifted, 1 - shifted)

    def score(tile, slot):
        phase, head, start = tile
        stop = start + TILE
        base = pl.multiple_of(halves[phase] * length + start, TILE)
        query = q_ref[pl.ds(base, TILE), head * head_dim : (head + 1) * head_dim]
        scores = dot(query, keys[halves[phase], :, :stop])
        row = lax.broadcasted_iota(jnp.int32, (TILE, TILE), 0)
        col = lax.broadcasted_iota(jnp.int32, (TILE, TILE), 1)
        last = jnp.where(row >= col, scores[:, start:], neg_big)
        top = jnp.max(last, axis=1, keepdims=True)
        score_bufs[slot][:, start:stop] = last
        if start:
            top = jnp.maximum(top, jnp.max(scores[:, :start], axis=1, keepdims=True))
            score_bufs[slot][:, :start] = scores[:, :start]
        return top

    def weigh(tile, top, slot):
        phase, head, start = tile
        stop = start + TILE
        weight_bufs[slot][:, :stop] = jnp.exp2((score_bufs[slot][:, :stop] - top) * factor).astype(bf16)
        return top

    def finish(tile, top, slot):
        phase, head, start = tile
        stop = start + TILE
        rows, cols = slice(start, stop), slice(head * head_dim, (head + 1) * head_dim)
        out = dot(weight_bufs[slot][:, :stop], values[halves[phase], :stop, :])
        if phase == 0:
            plain_ref[rows, cols] = (out[:, :head_dim] / out[:, head_dim:]).astype(bf16)
        else:
            part_ref[rows, cols] = out[:, :head_dim]
            stat_ref[rows, head : head + 1] = top
            stat_ref[rows, heads + head : heads + head + 1] = out[:, head_dim : head_dim + 1]

    tiles = [
        (phase, head, start)
        for phase in range(2) for head in range(heads) for start in range(0, length, TILE)
    ]
    pipeline(tiles, score, weigh, finish)
    act_ref[...] = dot(down_ref[...], plain_ref[...], ((1,), (1,)))


def cross_kernel(
    info, q_ref, own_ref, other_ref, ho_ref, hx_ref, part_ref, stat_ref,
    down_ref, plain_act_ref, back_ref, cross_ref, send_ref, keep_ref,
    keys, values, turn, s0, s1, p0, p1,
):
    shifted, core = info[0], info[1]
    head_dim = own_ref.shape[0]
    half_dim = head_dim // 2
    length = q_ref.shape[0] // 2
    heads = q_ref.shape[1] // head_dim
    rank = down_ref.shape[0]
    factor = math.log2(math.e) / math.sqrt(head_dim)
    score_bufs, weight_bufs = (s0, s1), (p0, p1)
    halo = shifted == 1
    load_keys(
        keys,
        jnp.where(halo, ho_ref[:half_dim, :], own_ref[:half_dim, :length]),
        jnp.where(halo, hx_ref[:half_dim, :], other_ref[:half_dim, :length]),
        core, half_dim,
    )
    load_keys(
        turn,
        jnp.where(halo, ho_ref[half_dim:, :], own_ref[half_dim:, :length]),
        jnp.where(halo, hx_ref[half_dim:, :], other_ref[half_dim:, :length]),
        core, half_dim,
    )
    load_values(values, turn, head_dim)

    def score(tile, slot):
        head, start = tile
        base = pl.multiple_of((1 - shifted) * length + start, TILE)
        query = q_ref[pl.ds(base, TILE), head * head_dim : (head + 1) * head_dim]
        scores = dot(query, keys[...])
        score_bufs[slot][...] = scores
        top = jnp.max(scores, axis=1, keepdims=True)
        return jnp.maximum(top, stat_ref[start : start + TILE, head : head + 1])

    def weigh(tile, top, slot):
        weight_bufs[slot][...] = jnp.exp2((score_bufs[slot][...] - top) * factor).astype(bf16)
        return top

    def finish(tile, top, slot):
        head, start = tile
        rows, cols = slice(start, start + TILE), slice(head * head_dim, (head + 1) * head_dim)
        out = dot(weight_bufs[slot][...], values[...])
        fade = jnp.exp2((stat_ref[rows, head : head + 1] - top) * factor)
        total = out[:, head_dim:] + fade * stat_ref[rows, heads + head : heads + head + 1]
        cross_ref[rows, cols] = (
            (out[:, :head_dim] + fade * part_ref[rows, cols]) / total
        ).astype(bf16)

    pipeline(
        [(head, start) for head in range(heads) for start in range(0, length, TILE)],
        score, weigh, finish,
    )
    cross = dot(down_ref[...], cross_ref[...], ((1,), (1,)))
    same = shifted == core
    plain = plain_act_ref[...]
    keep_ref[:rank, :] = jnp.where(same, plain, cross)
    send_ref[:rank, :] = jnp.where(same, cross, plain).astype(bf16)
    early, late = back_ref[:, :length], back_ref[:, length:]
    keep_ref[rank:, :] = jnp.where(core == 0, early, late)
    send_ref[rank:, :] = jnp.where(core == 0, late, early).astype(bf16)


def stage_kernel(k_hbm, v_hbm, halo_hbm, near, sems):
    rows, length = k_hbm.shape[0], halo_hbm.shape[1]
    sources = (k_hbm, v_hbm)
    spans = (slice(0, rows), slice(rows, 2 * rows))
    fetches = [
        pltpu.make_async_copy(source, near.at[span], sems.at[i])
        for i, (source, span) in enumerate(zip(sources, spans))
    ]
    stores = [
        pltpu.make_async_copy(near.at[span, length:], halo_hbm.at[span], sems.at[2 + i])
        for i, span in enumerate(spans)
    ]
    for fetch in fetches:
        fetch.start()
    for fetch, store in zip(fetches, stores):
        fetch.wait()
        store.start()
    for store in stores:
        store.wait()


def pair_sum_kernel(keep_ref, got_ref, out_ref):
    count, _, width = out_ref.shape
    for j in range(count):
        cols = slice(j * width, (j + 1) * width)
        out_ref[j] = (keep_ref[:, cols] + got_ref[:, cols].astype(f32)).astype(bf16)


def spread_sum_kernel(in_ref, out_ref, *, scale):
    count = in_ref.shape[0]
    total = in_ref[0].astype(f32)
    for j in range(1, count):
        total = total + in_ref[j].astype(f32)
    total = (total * scale).astype(out_ref.dtype)
    for j in range(count):
        out_ref[j] = total


def gradient_kernel(info, piece_ref, grad_ref, plain_ref, cross_ref, *rest, last):
    if last:
        before, act, *turns, low, back, whole = rest
    else:
        act, whole, low, back = rest
    shifted, core, row = info[0], info[1], info[2]
    count, rows, width = piece_ref.shape
    rank = rows // 2
    length = count * width
    half = 1 - core if last else core
    own = pl.ds(pl.multiple_of(half * length, length), length)
    for j in range(count):
        piece = piece_ref[j]
        cols = slice(j * width, (j + 1) * width)
        low[:, cols] = piece[:rank]
        back[:, cols] = piece[rank:]
        act[:, cols] = piece[:rank].astype(f32)
    attention = jnp.where(shifted == half, plain_ref[...], cross_ref[...])
    upper = dot(low[...], grad_ref[own, :])
    lower = dot(back[...], attention)
    if not last:
        whole[:rank, :] = upper
        whole[rank:, :] = lower
        return
    fine = rank // len(turns)
    for j in range(len(turns)):
        part = slice(j * fine, (j + 1) * fine)
        whole[j, :fine, :] = before[part, :] + upper[part, :]
        whole[j, fine:, :] = before[rank + j * fine : rank + (j + 1) * fine, :] + lower[part, :]
    for m, turn in enumerate(turns):
        turn[...] = whole[lax.rem(row + m, len(turns))]


def ring_sum_kernel(own_ref, one_ref, two_ref, three_ref, out_ref, *, scale):
    total = (own_ref[...] + two_ref[...]) + (one_ref[...] + three_ref[...])
    out_ref[...] = total * scale if scale != 1 else total


def place_kernel(info, *refs):
    *pieces, up_ref, down_ref = refs
    count = len(pieces)
    fine = pieces[0].shape[0] // 2
    for m, piece in enumerate(pieces):
        slot = lax.rem(info[2] + count - m, count)
        rows = pl.ds(pl.multiple_of(slot * fine, fine), fine)
        up_ref[rows, :] = piece[:fine, :]
        down_ref[rows, :] = piece[fine:, :]


def call(kernel, out_shape, operands, name, scalars=0, hbm=0, hbm_out=0, scratch=(), cost=None, limit=24):
    smem = pl.BlockSpec(memory_space=pltpu.SMEM)
    vmem = pl.BlockSpec(memory_space=pltpu.VMEM)
    far = pl.BlockSpec(memory_space=pltpu.HBM)
    return pl.pallas_call(
        kernel,
        out_shape=out_shape,
        in_specs=[smem] * scalars + [far] * hbm + [vmem] * (len(operands) - scalars - hbm),
        out_specs=[far] * hbm_out + [vmem] * (len(out_shape) - hbm_out)
        if isinstance(out_shape, list) else vmem,
        scratch_shapes=scratch,
        compiler_params=pltpu.CompilerParams(vmem_limit_bytes=limit << 20),
        cost_estimate=cost,
        name=name,
    )(*operands)


def shape(dims, dtype):
    return jax.ShapeDtypeStruct(dims, dtype)


def on_device(queries, keys, values, down, up, grad):
    core = lax.axis_index("core")
    zs = lax.axis_size("z")
    shifted = (lax.axis_index("z") < zs // 2).astype(jnp.int32)
    info = jnp.stack([shifted, core.astype(jnp.int32), lax.axis_index("x").astype(jnp.int32)])
    seq = lax.axis_size("x") * lax.axis_size("y")
    length, width = queries.shape
    half = length // 2
    half_dim = keys.shape[0]
    head_dim = 2 * half_dim
    heads = width // head_dim
    rank = up.shape[0]

    def to_partner(x):
        return lax.ppermute(x, "core", [(0, 1), (1, 0)])

    def far(x):
        return pltpu.with_memory_space_constraint(x, pltpu.HBM)

    later, pairs = call(
        stage_kernel,
        [shape((head_dim, half), bf16), shape((head_dim, length), bf16)],
        (far(keys), far(values)), "stage", hbm=2, hbm_out=1, limit=8,
        scratch=[pltpu.SemaphoreType.DMA((4,))],
        cost=pl.CostEstimate(flops=8 << 30, bytes_accessed=1 << 20, transcendentals=0),
    )
    pairs_other = to_partner(pairs)
    halo = lax.ppermute(later, ("x", "y"), [(i, (i + 1) % seq) for i in range(seq)])
    down_t = down.T

    tile_scratch = [
        pltpu.VMEM((TILE, half), f32), pltpu.VMEM((TILE, half), f32),
        pltpu.VMEM((TILE, half), bf16), pltpu.VMEM((TILE, half), bf16),
    ]
    cost = pl.CostEstimate(
        flops=4 * heads * half * half * head_dim, bytes_accessed=6 << 20,
        transcendentals=heads * half * half,
    )
    plain, act_plain, part, stat = call(
        diagonal_kernel,
        [
            shape((half, width), bf16), shape((rank, half), f32),
            shape((half, width), f32), shape((half, 2 * heads), f32),
        ],
        (info, queries, pairs, pairs_other, down_t),
        "diagonal", scalars=1, cost=cost,
        scratch=[
            pltpu.VMEM((2, head_dim, half), bf16),
            pltpu.VMEM((2, half, 2 * head_dim), bf16),
            pltpu.VMEM((head_dim, half), bf16),
        ] + tile_scratch,
    )
    halo, up, act_plain = lax.optimization_barrier((halo, up, act_plain))
    halo_other = to_partner(halo)
    back_part = dot(up, grad, ((1,), (1,)))
    cross, send, keep = call(
        cross_kernel,
        [shape((half, width), bf16), shape((2 * rank, half), bf16), shape((2 * rank, half), f32)],
        (info, queries, pairs, pairs_other, halo, halo_other, part, stat,
         down_t, act_plain, back_part),
        "cross", scalars=1, cost=cost,
        scratch=[
            pltpu.VMEM((head_dim, half), bf16),
            pltpu.VMEM((half, 2 * head_dim), bf16),
            pltpu.VMEM((head_dim, half), bf16),
        ] + tile_scratch,
    )

    got = to_partner(send)
    chunk = half // zs
    sent = call(pair_sum_kernel, shape((zs, 2 * rank, chunk), bf16), (keep, got), "pair_sum", limit=8)
    terms = lax.all_to_all(sent, "z", 0, 0)
    spread = call(
        lambda a, b: spread_sum_kernel(a, b, scale=1.0),
        shape((zs, 2 * rank, chunk), bf16), (terms,), "z_sum", limit=8,
    )
    own = lax.all_to_all(spread, "z", 0, 0)
    other = to_partner(own)
    side = lax.axis_size("y")
    grad_cost = pl.CostEstimate(
        flops=4 * rank * half * width, bytes_accessed=4 << 20, transcendentals=0
    )
    grad_scratch = [pltpu.VMEM((rank, half), bf16), pltpu.VMEM((rank, half), bf16)]
    act_own, factors = call(
        functools.partial(gradient_kernel, last=False),
        [shape((rank, half), f32), shape((2 * rank, width), f32)],
        (info, own, grad, plain, cross), "gradients_own", scalars=1, limit=16,
        scratch=grad_scratch, cost=grad_cost,
    )
    part_shape = (2 * rank // side, width)
    act_other, *turns = call(
        functools.partial(gradient_kernel, last=True),
        [shape((rank, half), f32)] + [shape(part_shape, f32)] * side,
        (info, other, grad, plain, cross, factors), "gradients_other", scalars=1, limit=16,
        scratch=grad_scratch + [pltpu.VMEM((side, *part_shape), f32)], cost=grad_cost,
    )
    activations = jnp.concatenate(
        [jnp.where(core == 0, act_own, act_other), jnp.where(core == 0, act_other, act_own)], axis=1
    )

    def passed(x, axis, steps):
        count = lax.axis_size(axis)
        return lax.ppermute(x, axis, [(i, (i + steps) % count) for i in range(count)])

    def exchanged(sent, axis):
        two = passed(sent[1], axis, 2)
        return passed(sent[0], axis, 1), two, passed(sent[2], axis, 3)

    def ring_sum(x, others, scale, name):
        return call(
            functools.partial(ring_sum_kernel, scale=scale), shape(part_shape, f32),
            (x, *others), name, limit=8,
        )

    sums = ring_sum(turns[0], exchanged(turns[1:], "x"), 1, "x_sum")
    sums = ring_sum(sums, exchanged([sums] * 3, "y"), adapter_scale, "y_sum")
    up_gradient, down_gradient = call(
        place_kernel, [shape((rank, width), f32)] * 2,
        (info, sums, *exchanged([sums] * 3, "x")), "place", scalars=1, limit=8,
    )
    return activations, down_gradient.T, up_gradient


def solution(mesh):
    devices = mesh.devices
    side = math.isqrt(devices.shape[0])
    split = Mesh(
        devices.reshape(side, side, devices.shape[1] // 2, 2), ("x", "y", "z", "core")
    )
    seq, head = ("x", "y"), ("z", "core")
    in_specs = (
        P(seq, head),
        P(head, seq),
        P(head, seq),
        P(head, None),
        P(None, head),
        P(seq, head),
    )
    out_specs = (P(None, seq), P(head, None), P(None, head))
    return jax.shard_map(
        on_device, mesh=split, in_specs=in_specs, out_specs=out_specs, check_vma=False
    )
```
